32 devices in a mesh: shots: 2 (over x), depth: 16 (over z, y, core).
Axes of the slice: x: 2, y: 2, z: 4, core: 2. Of those that a mesh axis runs over, the one named last changes fastest.
Arguments:
- fields_in: float32 [16, 4, 64, 2048], P('depth', None, 'shots'), parts along dimension 2, may hold values from -6 to 6
- flight_angular: float32 [16, 64], P('depth', 'shots'), parts along dimension 1, may hold values from 0.6 to 3
- wavelet: float32 [3, 2, 64], P(None, None, 'shots'), parts along dimension 2, may hold values from -6 to 6
- surface_angular: float32 [3, 64], P(None, 'shots'), parts along dimension 1, may hold values from 0.6 to 3
- records: float32 [3, 2, 64, 1024], P(None, None, 'shots'), parts along dimension 2, may hold values from -6 to 6
- source_pos: int32 [2], P('shots'), parts along dimension 0, may hold values from 0 to 2047
- receiver_pos: int32 [2048], P('shots'), parts along dimension 0, may hold values from 0 to 2047
- vel_table: float32 [64, 16], P('depth'), may hold values from 1.5 to 4.5
- vel_index: int32 [64, 2048], P('depth'), may hold values from 0 to 15
Outputs:
- section: float32 [64, 4096], P('depth', 'shots'), parts along dimension 1
- fields_out: float32 [16, 4, 64, 2048], P('depth', None, 'shots'), parts along dimension 2
The draws below stay inside these ranges and needn't reach their ends.
There are 2 independent parts, one for each index of `shots`. The reference program is written for one: setup_inputs(seed, part) draws one part's arguments, and reference() takes and returns one part's arrays. A program takes and returns all parts, laid end to end along the dimension named above; an argument that names none is the same for every part. Nothing has to cross between parts.
All inputs are finite; a program needn't handle non-finite values.
Results may differ from the reference program's by a relative error of at most 0.0003.
Values sent between devices are 32-bit elements; how exact they have to be, the bound alone decides.
A program may use at most 64 MiB of HBM per device.

```python
import math
import jax
import jax.numpy as jnp
from jax import lax

NX = 2048
FB = 32
NREC = 1024
LAYERS = 4
TICKS = 3
NV = 16
NZ = 64
N_DEPTH = 16


def plant(values, key, low, largest):
    index_at = [jax.random.randint(jax.random.fold_in(key, axis), (), 0, length) for axis, length in enumerate(values.shape)]
    main_axis = values.shape.index(max(values.shape))
    beside = index_at[:main_axis] + [(index_at[main_axis] + 1) % values.shape[main_axis]] + index_at[main_axis + 1:]
    return values.at[tuple(index_at)].set(low).at[tuple(beside)].set(largest)


def level_of(key, shape, shards, smallest, largest):
    loudness, own = 1.0, jax.random.fold_in(key, 6)
    for position, shards_of in shards:
        steps = jnp.exp(jax.random.uniform(jax.random.fold_in(own, position), (shards_of,), jnp.float32, smallest / len(shards), largest / len(shards)))
        loudness = loudness * jnp.repeat(steps, shape[position] // shards_of).reshape([-1 if axis == position else 1 for axis in range(len(shape))])
    return loudness


def scatter_about(own_key, dims, deviation, most, split=(), kind=jnp.bfloat16):
    gain = level_of(own_key, dims, split, -0.22, 0.18) if split else 1.0
    values = jax.random.normal(own_key, dims, jnp.float32) * deviation * gain
    return jnp.minimum(jnp.maximum(values, -most), most).astype(kind)


def setup_inputs(seed: int = 0, part: int = 0) -> dict:
    seeds = jax.random.split(jax.random.key(seed), 10)
    part_keys = jax.random.split(jax.random.fold_in(seeds[9], part), 10)
    fields_in = scatter_about(part_keys[0], (N_DEPTH, 4, FB, NX), 1.0, 6.0, ((0, 16),), jnp.float32)
    flight_angular = jnp.clip(0.6 + 2.4 * jax.random.uniform(part_keys[1], (N_DEPTH, FB), jnp.float32) ** level_of(part_keys[1], (N_DEPTH, FB), ((0, 16),), -0.2, 0.2), 0.6, 3.0)
    wavelet = scatter_about(part_keys[2], (TICKS, 2, FB), 1.0, 6.0, (), jnp.float32)
    surface_angular = jnp.clip(jax.random.uniform(part_keys[3], (TICKS, FB), jnp.float32, 0.6, 3.0), 0.6, 3.0)
    records = scatter_about(part_keys[4], (TICKS, 2, FB, NREC), 1.0, 6.0, (), jnp.float32)
    source_pos = jax.random.randint(part_keys[5], (1,), 0, NX).astype(jnp.int32)
    receiver_pos = plant(jax.random.randint(part_keys[6], (NREC,), 0, NX), jax.random.fold_in(part_keys[6], 1), 0, NX - 1).astype(jnp.int32)
    vel_table = jnp.clip(jnp.exp(math.log(4.5) - 1.0986123 * jax.random.uniform(seeds[7], (NZ, NV), jnp.float32) ** level_of(seeds[7], (NZ, NV), ((0, 16),), -0.2, 0.2)), 1.5, 4.5)
    vel_index = plant(jax.random.randint(seeds[8], (NZ, NX), 0, NV), jax.random.fold_in(seeds[8], 1), 0, NV - 1).astype(jnp.int32)
    return dict(fields_in=fields_in, flight_angular=flight_angular, wavelet=wavelet, surface_angular=surface_angular, records=records, source_pos=source_pos, receiver_pos=receiver_pos, vel_table=vel_table, vel_index=vel_index)


depth_step = 1.0
lateral_scale = 0.03
damping = 0.3

def lateral(values):
    padded = jnp.pad(values, [(0, 0)] * (values.ndim - 1) + [(2, 2)])
    return (16.0 * (padded[..., 1:-3] + padded[..., 3:-1]) - (padded[..., :-4] + padded[..., 4:]) - 30.0 * padded[..., 2:-2]) / 12.0

def layer_step(fields, angular, velocity):
    freq_col = angular[..., :, None]
    speed_row = velocity[..., None, :]
    phase_angle = freq_col * (depth_step / speed_row)
    cosine = jnp.cos(phase_angle)
    sine_part = jnp.sin(phase_angle)
    lateral_gain = lateral_scale * speed_row / (2.0 * freq_col)
    source_real = fields[..., 0, :, :]
    source_imag = fields[..., 1, :, :]
    receiver_real = fields[..., 2, :, :]
    receiver_imag = fields[..., 3, :, :]
    rotated = jnp.stack([source_real * cosine - source_imag * sine_part, source_real * sine_part + source_imag * cosine, receiver_real * cosine + receiver_imag * sine_part, receiver_imag * cosine - receiver_real * sine_part], axis=-3)
    spread = lateral(rotated)
    new_source_real = rotated[..., 0, :, :] + lateral_gain * (damping * spread[..., 0, :, :] - spread[..., 1, :, :])
    new_source_imag = rotated[..., 1, :, :] + lateral_gain * (damping * spread[..., 1, :, :] + spread[..., 0, :, :])
    new_receiver_real = rotated[..., 2, :, :] + lateral_gain * (damping * spread[..., 2, :, :] + spread[..., 3, :, :])
    new_receiver_imag = rotated[..., 3, :, :] + lateral_gain * (damping * spread[..., 3, :, :] - spread[..., 2, :, :])
    contrib = lax.optimization_barrier(jnp.sum(new_source_real * new_receiver_real + new_source_imag * new_receiver_imag, axis=-2)) * (1.0 / math.sqrt(FB))
    result = jnp.stack([new_source_real, new_source_imag, new_receiver_real, new_receiver_imag], axis=-3)
    return (result, contrib)

def surface_block(period, wavelet, surface_angular, records, source_pos, receiver_pos, width):
    lateral_cells = jnp.arange(width, dtype=jnp.int32)
    source_spot = (lateral_cells == source_pos[0]).astype(jnp.float32)
    source_field = wavelet[period][:, :, None] * source_spot
    receiver_field = jnp.zeros((2, wavelet.shape[2], width), jnp.float32).at[:, :, receiver_pos].add(records[period])
    return (jnp.concatenate([source_field, receiver_field], 0), surface_angular[period])

def reference(fields_in, flight_angular, wavelet, surface_angular, records, source_pos, receiver_pos, vel_table, vel_index):
    chain = fields_in.shape[0]
    width = fields_in.shape[3]
    velocity = jnp.take_along_axis(vel_table, vel_index, axis=1).reshape(chain, LAYERS, width)
    fields = fields_in
    angular = flight_angular
    section = jnp.zeros((chain, LAYERS, width), jnp.float32)
    for period in range(TICKS):
        layer_rows = []
        for stratum in range(LAYERS):
            fields, contrib = layer_step(fields, angular, velocity[:, stratum])
            layer_rows.append(contrib)
        section = section + jnp.stack(layer_rows, 1)
        top_fields, top_angular = surface_block(period, wavelet, surface_angular, records, source_pos, receiver_pos, width)
        fields = jnp.concatenate([top_fields[None], fields[:-1]], 0)
        angular = jnp.concatenate([top_angular[None], angular[:-1]], 0)
    stacked = section.reshape(chain * LAYERS, width)
    padded = jnp.pad(stacked, ((1, 1), (0, 0)))
    filtered = 2.0 * stacked - 0.5 * (padded[:-2] + padded[2:])
    return (filtered, fields)
```

```python
import functools
import math

import jax
import jax.numpy as jnp
from jax import lax
from jax.experimental import pallas as pl
from jax.experimental.pallas import tpu as pltpu
from jax.sharding import PartitionSpec as P

FB = 32
TICKS = 3
LAYERS = 4
SUB = 8
LANE = 128
GROUPS = FB // SUB

lateral_scale = 0.03
damping = 0.3

COS = (1.0, -0.4999999403953552, 0.041666459292173386, -0.0013886659871786833, 2.4693899831618182e-05, -2.514234438422136e-07)
SINC = (0.9999999403953552, -0.16666607558727264, 0.008332140743732452, -0.00019757583504542708, 2.5143860966636566e-06)


def poly(y, coefs):
    acc = coefs[-1] * y + coefs[-2]
    for c in coefs[-3::-1]:
        acc = acc * y + c
    return acc


def as_column(row):
    size = row.shape[1]
    diag = lax.broadcasted_iota(jnp.int32, (size, size), 0) == lax.broadcasted_iota(jnp.int32, (size, size), 1)
    return jnp.sum(jnp.where(diag, row, 0.0), axis=1, keepdims=True)


def kernel(
    n, fin, fang, wav, sang, rec, spos, rpos, vtab, vidx,
    fout, section,
    work, surf, recbuf, wb, vel, wide, rwide, cacc, up1, own4, dn4, dn8, dn12, in_up, in_dn4, in_dn8, in_dn12,
    fin_sem, rec_sem, top_sem, vsend, vrecv, fsend, frecv, isend, irecv,
):
    width = fin.shape[3]
    cols = width // LANE
    d = lax.axis_index("depth")

    def at(k):
        return {"depth": lax.rem(d + k + n, n)}

    barrier = pltpu.get_barrier_semaphore()
    for k in (1, 2, 3, -1, -2, -3):
        pl.semaphore_signal(barrier, inc=1, device_id=at(k), device_id_type=pl.DeviceIdType.MESH)

    def fin_copy(g):
        rows = pl.ds(pl.multiple_of(g * SUB, SUB), SUB)
        return pltpu.make_async_copy(fin.at[0, :, rows, :], work.at[:, rows, :], fin_sem.at[g])

    for g in range(GROUPS):
        fin_copy(g).start()

    has_top = jnp.logical_or(d == 0, d >= n - 2)
    tick = jnp.where(d == 0, TICKS - 1, lax.rem(n - 1 - d, TICKS))
    rec_copy = pltpu.make_async_copy(rec.at[tick], recbuf, rec_sem.at[0])

    @pl.when(has_top)
    def _():
        rec_copy.start()

    def spread_rows(j):
        speeds = vel[j]
        slow = 1.0 / speeds
        for k in range(LAYERS):
            wide[j * LAYERS + k] = jnp.broadcast_to(speeds[k:k + 1, :], (SUB, width))
            rwide[j * LAYERS + k] = jnp.broadcast_to(slow[k:k + 1, :], (SUB, width))

    index = vidx[...]
    speed = jnp.zeros(index.shape, jnp.float32)
    for i in range(vtab.shape[1]):
        speed = jnp.where(index == i, vtab[:, i:i + 1], speed)
    vel[0] = speed
    spread_rows(0)

    pl.semaphore_wait(barrier, 6)

    def vel_copy(j):
        return pltpu.make_async_remote_copy(
            src_ref=vel.at[0], dst_ref=vel.at[j], send_sem=vsend.at[j], recv_sem=vrecv.at[j],
            device_id=at(-j), device_id_type=pl.DeviceIdType.MESH)

    vel_copy(1).start()
    vel_copy(2).start()

    wb[0] = jnp.broadcast_to(as_column(fang[...]), (FB, LANE))
    cacc[...] = jnp.zeros_like(cacc)

    @pl.when(has_top)
    def _():
        wb[1] = jnp.broadcast_to(as_column(sang[pl.ds(tick, 1), :]), (FB, LANE))
        cell = lax.broadcasted_iota(jnp.int32, (FB, width), 1)
        pair = wav[tick]
        for i in range(2):
            surf[i] = jnp.where(cell == spos[0], as_column(pair[i:i + 1, :]), 0.0)
        rec_copy.wait()
        values = recbuf[...].reshape(2 * FB, recbuf.shape[2])
        high = values.astype(jnp.bfloat16)
        rest = values - high.astype(jnp.float32)
        mid = rest.astype(jnp.bfloat16)
        low = (rest - mid.astype(jnp.float32)).astype(jnp.bfloat16)
        parts = jnp.concatenate([high, mid, low], axis=0)
        where_to = rpos[...]
        block = 2 * LANE

        def place(i, carry):
            first = pl.multiple_of(i * block, block)
            x = lax.broadcasted_iota(jnp.int32, (block, where_to.shape[1]), 0) + first
            hit = jnp.where(x == where_to, 1.0, 0.0).astype(jnp.bfloat16)
            got = lax.dot_general(parts, hit, (((1,), (1,)), ((), ())), preferred_element_type=jnp.float32)
            total = got[:2 * FB] + (got[2 * FB:4 * FB] + got[4 * FB:])
            surf[2:4, :, pl.ds(first, block)] = total.reshape(2, FB, block)
            return carry

        lax.fori_loop(0, width // block, place, 0)

    top_copy = pltpu.make_async_copy(surf, fout.at[0], top_sem.at[0])

    @pl.when(d == 0)
    def _():
        top_copy.start()

    lane = lax.broadcasted_iota(jnp.int32, (SUB, LANE), 1)
    zero = jnp.zeros((SUB, LANE), jnp.float32)

    def layer(g, j, l):
        rows = pl.ds(pl.multiple_of(g * SUB, SUB), SUB)
        w = wb[jnp.where(d + j >= n, 1, 0), rows, :]
        gain_w = (lateral_scale * 16.0 / 24.0) / w
        keep_l1, keep_l2 = lane < 1, lane < 2
        keep_r1, keep_r2 = lane >= LANE - 1, lane >= LANE - 2

        def rotated(c):
            span = pl.ds(c * LANE, LANE)
            p = w * rwide[j * LAYERS + l, :, span]
            y = p * p
            co = poly(y, COS)
            si = p * poly(y, SINC)
            sr, sm = work[0, rows, span], work[1, rows, span]
            rr, rm = work[2, rows, span], work[3, rows, span]
            u = (sr * co - sm * si, sr * si + sm * co, rr * co + rm * si, rm * co - rr * si)
            return [(v, pltpu.roll(v, 1, 1), pltpu.roll(v, 2, 1), pltpu.roll(v, LANE - 1, 1), pltpu.roll(v, LANE - 2, 1)) for v in u]

        outside = [(zero,) * 5] * 4
        before, here = outside, rotated(0)
        for c in range(cols):
            after = rotated(c + 1) if c + 1 < cols else outside
            span = pl.ds(c * LANE, LANE)
            spread = []
            for q in range(4):
                left1 = jnp.where(keep_l1, before[q][1], here[q][1])
                left2 = jnp.where(keep_l2, before[q][2], here[q][2])
                right1 = jnp.where(keep_r1, after[q][3], here[q][3])
                right2 = jnp.where(keep_r2, after[q][4], here[q][4])
                spread.append((left1 + right1) - (left2 + right2) * (1.0 / 16.0) - here[q][0] * 1.875)
            gain = gain_w * wide[j * LAYERS + l, :, span]
            damp = gain * damping
            new = (
                here[0][0] + (damp * spread[0] - gain * spread[1]),
                here[1][0] + (damp * spread[1] + gain * spread[0]),
                here[2][0] + (damp * spread[2] + gain * spread[3]),
                here[3][0] + (damp * spread[3] - gain * spread[2]),
            )
            for q in range(4):
                work[q, rows, span] = new[q]
            k = j * LAYERS + l
            cacc[k, :, span] = cacc[k, :, span] + (new[0] * new[2] + new[1] * new[3])
            before, here = here, after

    def out_copy(g):
        rows = pl.ds(pl.multiple_of(g * SUB, SUB), SUB)
        return pltpu.make_async_remote_copy(
            src_ref=work.at[:, rows, :], dst_ref=fout.at[0, :, rows, :],
            send_sem=fsend.at[g], recv_sem=frecv.at[g],
            device_id=at(3), device_id_type=pl.DeviceIdType.MESH)

    def group(g, carry):
        rows = pl.ds(pl.multiple_of(g * SUB, SUB), SUB)
        fin_copy(g).wait()

        def slab(j, carry):
            @pl.when(jnp.logical_and(g == 0, j > 0))
            def _():
                vel_copy(j).wait_recv()
                spread_rows(j)

            @pl.when(jnp.logical_and(j > 0, d + j == n))
            def _():
                work[:, rows, :] = surf[:, rows, :]

            def one(l, carry):
                layer(g, j, l)
                return carry

            return lax.fori_loop(0, LAYERS, one, carry)

        lax.fori_loop(0, TICKS, slab, 0)

        @pl.when(d != n - 3)
        def _():
            out_copy(g).start()

        return carry

    lax.fori_loop(0, GROUPS, group, 0)

    joined = [jnp.where(lax.rem(d + k, n) == 0, 0.0, 0.5).astype(jnp.float32) for k in range(4)]
    last = TICKS * LAYERS
    rows = [jnp.sum(cacc[k], axis=0, keepdims=True) * (1.0 / math.sqrt(FB)) for k in range(last)]

    def filtered(k):
        total = 2.0 * rows[k]
        if k > 0:
            total = total - (joined[k // LAYERS] if k % LAYERS == 0 else 0.5) * rows[k - 1]
        if k + 1 < last:
            total = total - (joined[(k + 1) // LAYERS] if (k + 1) % LAYERS == 0 else 0.5) * rows[k + 1]
        return total

    up1[...] = -joined[0] * rows[0]
    dn12[...] = -joined[3] * rows[last - 1]
    for k in range(LAYERS):
        own4[pl.ds(k, 1), :] = filtered(k)
        dn4[pl.ds(k, 1), :] = filtered(LAYERS + k)
        dn8[pl.ds(k, 1), :] = filtered(2 * LAYERS + k)

    image_copies = [
        pltpu.make_async_remote_copy(
            src_ref=src, dst_ref=dst, send_sem=isend.at[i], recv_sem=irecv.at[i],
            device_id=at(k), device_id_type=pl.DeviceIdType.MESH)
        for i, (src, dst, k) in enumerate(((up1, in_up, -1), (dn4, in_dn4, 1), (dn8, in_dn8, 2), (dn12, in_dn12, 3)))
    ]
    for copy in image_copies:
        copy.start()
    for copy in image_copies:
        copy.wait()
    section[...] = own4[...] + in_dn4[...] + in_dn8[...]
    section[0:1, :] = section[0:1, :] + in_dn12[...]
    section[LAYERS - 1:LAYERS, :] = section[LAYERS - 1:LAYERS, :] + in_up[...]

    vel_copy(1).wait_send()
    vel_copy(2).wait_send()

    @pl.when(d != n - 3)
    def _():
        for g in range(GROUPS):
            out_copy(g).wait_send()

    @pl.when(d != 0)
    def _():
        for g in range(GROUPS):
            out_copy(g).wait_recv()

    @pl.when(d == 0)
    def _():
        top_copy.wait()


def on_device(n, fields_in, flight_angular, wavelet, surface_angular, records, source_pos, receiver_pos, vel_table, vel_index):
    width = fields_in.shape[3]
    f32 = jnp.float32
    vmem = pl.BlockSpec(memory_space=pltpu.VMEM)
    hbm = pl.BlockSpec(memory_space=pl.ANY)
    dma = pltpu.SemaphoreType.DMA
    last = TICKS * LAYERS
    fields_out, section = pl.pallas_call(
        functools.partial(kernel, n),
        out_shape=(
            jax.ShapeDtypeStruct(fields_in.shape, f32),
            jax.ShapeDtypeStruct((LAYERS, width), f32),
        ),
        in_specs=[hbm, vmem, vmem, vmem, hbm, pl.BlockSpec(memory_space=pltpu.SMEM), vmem, vmem, vmem],
        out_specs=(hbm, vmem),
        scratch_shapes=[
            pltpu.VMEM((4, FB, width), f32),
            pltpu.VMEM((4, FB, width), f32),
            pltpu.VMEM(records.shape[1:], f32),
            pltpu.VMEM((2, FB, LANE), f32),
            pltpu.VMEM((TICKS, LAYERS, width), f32),
            pltpu.VMEM((last, SUB, width), f32),
            pltpu.VMEM((last, SUB, width), f32),
            pltpu.VMEM((last, SUB, width), f32),
            pltpu.VMEM((1, width), f32),
            pltpu.VMEM((LAYERS, width), f32),
            pltpu.VMEM((LAYERS, width), f32),
            pltpu.VMEM((LAYERS, width), f32),
            pltpu.VMEM((1, width), f32),
            pltpu.VMEM((1, width), f32),
            pltpu.VMEM((LAYERS, width), f32),
            pltpu.VMEM((LAYERS, width), f32),
            pltpu.VMEM((1, width), f32),
            dma((GROUPS,)), dma((1,)), dma((1,)), dma((TICKS,)), dma((TICKS,)),
            dma((GROUPS,)), dma((GROUPS,)), dma((4,)), dma((4,)),
        ],
        compiler_params=pltpu.CompilerParams(
            collective_id=0, has_side_effects=True, vmem_limit_bytes=32 * 1024 * 1024),
        name="migrate",
    )(fields_in, flight_angular, wavelet, surface_angular, records, source_pos, receiver_pos.reshape(1, -1), vel_table, vel_index)
    return section, fields_out


def solution(mesh):
    placed = (
        P("depth", None, "shots", None),
        P("depth", "shots"),
        P(None, None, "shots"),
        P(None, "shots"),
        P(None, None, "shots", None),
        P("shots"),
        P("shots"),
        P("depth", None),
        P("depth", None),
    )
    return jax.shard_map(
        functools.partial(on_device, mesh.shape["depth"]),
        mesh=mesh,
        in_specs=placed,
        out_specs=(P("depth", "shots"), P("depth", None, "shots", None)),
        check_vma=False,
    )
```

```python
import functools
import math

import jax
import jax.numpy as jnp
from jax import lax
from jax.experimental import pallas as pl
from jax.experimental.pallas import tpu as pltpu
from jax.sharding import PartitionSpec as P

FB = 32
TICKS = 3
LAYERS = 4
SUB = 8
LANE = 128
GROUPS = FB // SUB

lateral_scale = 0.03
damping = 0.3

COS = (1.0, -0.4999999403953552, 0.041666459292173386, -0.0013886659871786833, 2.4693899831618182e-05, -2.514234438422136e-07)
SINC = (0.9999999403953552, -0.16666607558727264, 0.008332140743732452, -0.00019757583504542708, 2.5143860966636566e-06)


def poly(y, coefs):
    acc = coefs[-1] * y + coefs[-2]
    for c in coefs[-3::-1]:
        acc = acc * y + c
    return acc


def as_column(row):
    size = row.shape[1]
    diag = lax.broadcasted_iota(jnp.int32, (size, size), 0) == lax.broadcasted_iota(jnp.int32, (size, size), 1)
    return jnp.sum(jnp.where(diag, row, 0.0), axis=1, keepdims=True)


def kernel(
    n, fin, fang_in, wav_in, sang_in, rec, spos_in, rpos_in, vtab_in, vidx_in,
    fout, section_out,
    fang, wav, sang, spos, rpos, vtab, vidx, section,
    work, surf, recbuf, wb, vel, wide, rwide, cacc, up1, own4, dn4, dn8, dn12, in_up, in_dn4, in_dn8, in_dn12,
    small_sem, fin_sem, rec_sem, top_sem, vsend, vrecv, fsend, frecv, isend, irecv,
):
    width = fin.shape[3]
    cols = width // LANE
    d = lax.axis_index("depth")

    def at(k):
        return {"depth": lax.rem(d + k + n, n)}

    barrier = pltpu.get_barrier_semaphore()
    for k in (1, 2, 3, -1, -2, -3):
        pl.semaphore_signal(barrier, inc=1, device_id=at(k), device_id_type=pl.DeviceIdType.MESH)

    smalls = [
        pltpu.make_async_copy(src, dst, small_sem.at[i])
        for i, (src, dst) in enumerate((
            (vidx_in, vidx), (vtab_in, vtab), (fang_in, fang), (sang_in, sang), (wav_in, wav), (spos_in, spos), (rpos_in, rpos)))
    ]
    for copy in smalls:
        copy.start()

    def fin_copy(g):
        rows = pl.ds(pl.multiple_of(g * SUB, SUB), SUB)
        return pltpu.make_async_copy(fin.at[0, :, rows, :], work.at[:, rows, :], fin_sem.at[g])

    for g in range(GROUPS):
        fin_copy(g).start()

    has_top = jnp.logical_or(d == 0, d >= n - 2)
    tick = jnp.where(d == 0, TICKS - 1, lax.rem(n - 1 - d, TICKS))
    rec_copy = pltpu.make_async_copy(rec.at[tick], recbuf, rec_sem.at[0])

    @pl.when(has_top)
    def _():
        rec_copy.start()

    def spread_rows(j):
        speeds = vel[j]
        slow = 1.0 / speeds
        for k in range(LAYERS):
            wide[j * LAYERS + k] = jnp.broadcast_to(speeds[k:k + 1, :], (SUB, width))
            rwide[j * LAYERS + k] = jnp.broadcast_to(slow[k:k + 1, :], (SUB, width))

    smalls[0].wait()
    smalls[1].wait()
    index = vidx[...]
    speed = jnp.zeros(index.shape, jnp.float32)
    for i in range(vtab.shape[1]):
        speed = jnp.where(index == i, vtab[:, i:i + 1], speed)
    vel[0] = speed
    spread_rows(0)

    pl.semaphore_wait(barrier, 6)

    def vel_copy(j):
        return pltpu.make_async_remote_copy(
            src_ref=vel.at[0], dst_ref=vel.at[j], send_sem=vsend.at[j], recv_sem=vrecv.at[j],
            device_id=at(-j), device_id_type=pl.DeviceIdType.MESH)

    vel_copy(1).start()
    vel_copy(2).start()

    for copy in smalls[2:]:
        copy.wait()
    wb[0] = jnp.broadcast_to(as_column(fang[...]), (FB, LANE))
    cacc[...] = jnp.zeros_like(cacc)

    @pl.when(has_top)
    def _():
        wb[1] = jnp.broadcast_to(as_column(sang[pl.ds(tick, 1), :]), (FB, LANE))
        cell = lax.broadcasted_iota(jnp.int32, (FB, width), 1)
        pair = wav[tick]
        for i in range(2):
            surf[i] = jnp.where(cell == spos[...], as_column(pair[i:i + 1, :]), 0.0)
        rec_copy.wait()
        values = recbuf[...].reshape(2 * FB, recbuf.shape[2])
        high = values.astype(jnp.bfloat16)
        rest = values - high.astype(jnp.float32)
        mid = rest.astype(jnp.bfloat16)
        low = (rest - mid.astype(jnp.float32)).astype(jnp.bfloat16)
        parts = jnp.concatenate([high, mid, low], axis=0)
        where_to = rpos[...]
        block = 2 * LANE

        def place(i, carry):
            first = pl.multiple_of(i * block, block)
            x = lax.broadcasted_iota(jnp.int32, (block, where_to.shape[1]), 0) + first
            hit = jnp.where(x == where_to, 1.0, 0.0).astype(jnp.bfloat16)
            got = lax.dot_general(parts, hit, (((1,), (1,)), ((), ())), preferred_element_type=jnp.float32)
            total = got[:2 * FB] + (got[2 * FB:4 * FB] + got[4 * FB:])
            surf[2:4, :, pl.ds(first, block)] = total.reshape(2, FB, block)
            return carry

        lax.fori_loop(0, width // block, place, 0)

    top_copy = pltpu.make_async_copy(surf, fout.at[0], top_sem.at[0])

    @pl.when(d == 0)
    def _():
        top_copy.start()

    lane = lax.broadcasted_iota(jnp.int32, (SUB, LANE), 1)
    zero = jnp.zeros((SUB, LANE), jnp.float32)

    def layer(g, j, l):
        rows = pl.ds(pl.multiple_of(g * SUB, SUB), SUB)
        w = wb[jnp.where(d + j >= n, 1, 0), rows, :]
        gain_w = (lateral_scale * 16.0 / 24.0) / w
        keep_l1, keep_l2 = lane < 1, lane < 2
        keep_r1, keep_r2 = lane >= LANE - 1, lane >= LANE - 2

        def rotated(c):
            span = pl.ds(c * LANE, LANE)
            p = w * rwide[j * LAYERS + l, :, span]
            y = p * p
            co = poly(y, COS)
            si = p * poly(y, SINC)
            sr, sm = work[0, rows, span], work[1, rows, span]
            rr, rm = work[2, rows, span], work[3, rows, span]
            u = (sr * co - sm * si, sr * si + sm * co, rr * co + rm * si, rm * co - rr * si)
            return [(v, pltpu.roll(v, 1, 1), pltpu.roll(v, 2, 1), pltpu.roll(v, LANE - 1, 1), pltpu.roll(v, LANE - 2, 1)) for v in u]

        outside = [(zero,) * 5] * 4
        before, here = outside, rotated(0)
        for c in range(cols):
            after = rotated(c + 1) if c + 1 < cols else outside
            span = pl.ds(c * LANE, LANE)
            spread = []
            for q in range(4):
                left1 = jnp.where(keep_l1, before[q][1], here[q][1])
                left2 = jnp.where(keep_l2, before[q][2], here[q][2])
                right1 = jnp.where(keep_r1, after[q][3], here[q][3])
                right2 = jnp.where(keep_r2, after[q][4], here[q][4])
                spread.append((left1 + right1) - (left2 + right2) * (1.0 / 16.0) - here[q][0] * 1.875)
            gain = gain_w * wide[j * LAYERS + l, :, span]
            damp = gain * damping
            new = (
                here[0][0] + (damp * spread[0] - gain * spread[1]),
                here[1][0] + (damp * spread[1] + gain * spread[0]),
                here[2][0] + (damp * spread[2] + gain * spread[3]),
                here[3][0] + (damp * spread[3] - gain * spread[2]),
            )
            for q in range(4):
                work[q, rows, span] = new[q]
            k = j * LAYERS + l
            cacc[k, :, span] = cacc[k, :, span] + (new[0] * new[2] + new[1] * new[3])
            before, here = here, after

    def out_copy(g):
        rows = pl.ds(pl.multiple_of(g * SUB, SUB), SUB)
        return pltpu.make_async_remote_copy(
            src_ref=work.at[:, rows, :], dst_ref=fout.at[0, :, rows, :],
            send_sem=fsend.at[g], recv_sem=frecv.at[g],
            device_id=at(3), device_id_type=pl.DeviceIdType.MESH)

    def group(g, carry):
        rows = pl.ds(pl.multiple_of(g * SUB, SUB), SUB)
        fin_copy(g).wait()

        def slab(j, carry):
            @pl.when(jnp.logical_and(g == 0, j > 0))
            def _():
                vel_copy(j).wait_recv()
                spread_rows(j)

            @pl.when(jnp.logical_and(j > 0, d + j == n))
            def _():
                work[:, rows, :] = surf[:, rows, :]

            def one(l, carry):
                layer(g, j, l)
                return carry

            return lax.fori_loop(0, LAYERS, one, carry)

        lax.fori_loop(0, TICKS, slab, 0)

        @pl.when(d != n - 3)
        def _():
            out_copy(g).start()

        return carry

    lax.fori_loop(0, GROUPS, group, 0)

    joined = [jnp.where(lax.rem(d + k, n) == 0, 0.0, 0.5).astype(jnp.float32) for k in range(4)]
    last = TICKS * LAYERS
    rows = [jnp.sum(cacc[k], axis=0, keepdims=True) * (1.0 / math.sqrt(FB)) for k in range(last)]

    def filtered(k):
        total = 2.0 * rows[k]
        if k > 0:
            total = total - (joined[k // LAYERS] if k % LAYERS == 0 else 0.5) * rows[k - 1]
        if k + 1 < last:
            total = total - (joined[(k + 1) // LAYERS] if (k + 1) % LAYERS == 0 else 0.5) * rows[k + 1]
        return total

    up1[...] = -joined[0] * rows[0]
    dn12[...] = -joined[3] * rows[last - 1]
    for k in range(LAYERS):
        own4[pl.ds(k, 1), :] = filtered(k)
        dn4[pl.ds(k, 1), :] = filtered(LAYERS + k)
        dn8[pl.ds(k, 1), :] = filtered(2 * LAYERS + k)

    image_copies = [
        pltpu.make_async_remote_copy(
            src_ref=src, dst_ref=dst, send_sem=isend.at[i], recv_sem=irecv.at[i],
            device_id=at(k), device_id_type=pl.DeviceIdType.MESH)
        for i, (src, dst, k) in enumerate(((up1, in_up, -1), (dn4, in_dn4, 1), (dn8, in_dn8, 2), (dn12, in_dn12, 3)))
    ]
    for copy in image_copies:
        copy.start()
    for copy in image_copies:
        copy.wait()
    section[...] = own4[...] + in_dn4[...] + in_dn8[...]
    section[0:1, :] = section[0:1, :] + in_dn12[...]
    section[LAYERS - 1:LAYERS, :] = section[LAYERS - 1:LAYERS, :] + in_up[...]

    section_copy = pltpu.make_async_copy(section, section_out, small_sem.at[0])
    section_copy.start()
    section_copy.wait()
    vel_copy(1).wait_send()
    vel_copy(2).wait_send()

    @pl.when(d != n - 3)
    def _():
        for g in range(GROUPS):
            out_copy(g).wait_send()

    @pl.when(d != 0)
    def _():
        for g in range(GROUPS):
            out_copy(g).wait_recv()

    @pl.when(d == 0)
    def _():
        top_copy.wait()


def on_device(n, fields_in, flight_angular, wavelet, surface_angular, records, source_pos, receiver_pos, vel_table, vel_index):
    width = fields_in.shape[3]
    f32 = jnp.float32
    hbm = pl.BlockSpec(memory_space=pltpu.HBM)
    dma = pltpu.SemaphoreType.DMA
    last = TICKS * LAYERS
    fields_out, section = pl.pallas_call(
        functools.partial(kernel, n),
        out_shape=(
            jax.ShapeDtypeStruct(fields_in.shape, f32),
            jax.ShapeDtypeStruct((LAYERS, width), f32),
        ),
        in_specs=[hbm] * 9,
        out_specs=(hbm, hbm),
        scratch_shapes=[
            pltpu.VMEM(flight_angular.shape, f32),
            pltpu.VMEM(wavelet.shape, f32),
            pltpu.VMEM(surface_angular.shape, f32),
            pltpu.VMEM((1, 1), jnp.int32),
            pltpu.VMEM((1, receiver_pos.shape[0]), jnp.int32),
            pltpu.VMEM(vel_table.shape, f32),
            pltpu.VMEM(vel_index.shape, jnp.int32),
            pltpu.VMEM((LAYERS, width), f32),
            pltpu.VMEM((4, FB, width), f32),
            pltpu.VMEM((4, FB, width), f32),
            pltpu.VMEM(records.shape[1:], f32),
            pltpu.VMEM((2, FB, LANE), f32),
            pltpu.VMEM((TICKS, LAYERS, width), f32),
            pltpu.VMEM((last, SUB, width), f32),
            pltpu.VMEM((last, SUB, width), f32),
            pltpu.VMEM((last, SUB, width), f32),
            pltpu.VMEM((1, width), f32),
            pltpu.VMEM((LAYERS, width), f32),
            pltpu.VMEM((LAYERS, width), f32),
            pltpu.VMEM((LAYERS, width), f32),
            pltpu.VMEM((1, width), f32),
            pltpu.VMEM((1, width), f32),
            pltpu.VMEM((LAYERS, width), f32),
            pltpu.VMEM((LAYERS, width), f32),
            pltpu.VMEM((1, width), f32),
            dma((7,)), dma((GROUPS,)), dma((1,)), dma((1,)), dma((TICKS,)), dma((TICKS,)),
            dma((GROUPS,)), dma((GROUPS,)), dma((4,)), dma((4,)),
        ],
        compiler_params=pltpu.CompilerParams(
            collective_id=0, has_side_effects=True, vmem_limit_bytes=62 * 1024 * 1024),
        name="migrate",
    )(fields_in, flight_angular, wavelet, surface_angular, records, source_pos.reshape(1, 1), receiver_pos.reshape(1, -1), vel_table, vel_index)
    return section, fields_out


def solution(mesh):
    placed = (
        P("depth", None, "shots", None),
        P("depth", "shots"),
        P(None, None, "shots"),
        P(None, "shots"),
        P(None, None, "shots", None),
        P("shots"),
        P("shots"),
        P("depth", None),
        P("depth", None),
    )
    return jax.shard_map(
        functools.partial(on_device, mesh.shape["depth"]),
        mesh=mesh,
        in_specs=placed,
        out_specs=(P("depth", "shots"), P("depth", None, "shots", None)),
        check_vma=False,
    )
```

```python
import functools
import math

import jax
import jax.numpy as jnp
from jax import lax
from jax.experimental import pallas as pl
from jax.experimental.pallas import tpu as pltpu
from jax.sharding import PartitionSpec as P

FB = 32
TICKS = 3
LAYERS = 4
SUB = 8
LANE = 128
GROUPS = FB // SUB

lateral_scale = 0.03
damping = 0.3

COS = (1.0, -0.4999999403953552, 0.041666459292173386, -0.0013886659871786833, 2.4693899831618182e-05, -2.514234438422136e-07)
SINC = (0.9999999403953552, -0.16666607558727264, 0.008332140743732452, -0.00019757583504542708, 2.5143860966636566e-06)


def poly(y, coefs):
    acc = coefs[-1] * y + coefs[-2]
    for c in coefs[-3::-1]:
        acc = acc * y + c
    return acc


def as_column(row):
    size = row.shape[1]
    diag = lax.broadcasted_iota(jnp.int32, (size, size), 0) == lax.broadcasted_iota(jnp.int32, (size, size), 1)
    return jnp.sum(jnp.where(diag, row, 0.0), axis=1, keepdims=True)


def kernel(
    n, fin, fang_in, wav_in, sang_in, rec, spos_in, rpos_in, vtab_in, vidx_in,
    fout, section_out,
    fang, wav, sang, spos, rpos, vtab, vidx, section,
    field, recbuf, wb, vel, wide, rwide, cacc, up1, own4, dn4, dn8, dn12, in_up, in_dn4, in_dn8, in_dn12,
    small_sem, fin_sem, rec_sem, top_sem, vsend, vrecv, fsend, frecv, isend, irecv,
):
    width = fin.shape[3]
    cols = width // LANE
    d = lax.axis_index("depth")

    def at(k):
        return {"depth": lax.rem(d + k + n, n)}

    barrier = pltpu.get_barrier_semaphore()
    for k in (1, 2, 3, -1, -2, -3):
        pl.semaphore_signal(barrier, inc=1, device_id=at(k), device_id_type=pl.DeviceIdType.MESH)

    smalls = [
        pltpu.make_async_copy(src, dst, small_sem.at[i])
        for i, (src, dst) in enumerate((
            (vidx_in, vidx), (vtab_in, vtab), (fang_in, fang), (sang_in, sang), (wav_in, wav), (spos_in, spos), (rpos_in, rpos)))
    ]
    for copy in smalls:
        copy.start()

    def fin_copy(g):
        rows = pl.ds(pl.multiple_of(g * SUB, SUB), SUB)
        return pltpu.make_async_copy(fin.at[0, :, rows, :], field.at[0, :, rows, :], fin_sem.at[g])

    for g in range(GROUPS):
        fin_copy(g).start()

    has_top = jnp.logical_or(d == 0, d >= n - 2)
    tick = jnp.where(d == 0, TICKS - 1, lax.rem(n - 1 - d, TICKS))
    rec_copy = pltpu.make_async_copy(rec.at[tick], recbuf, rec_sem.at[0])

    @pl.when(has_top)
    def _():
        rec_copy.start()

    def spread_rows(j):
        speeds = vel[j]
        slow = 1.0 / speeds
        for k in range(LAYERS):
            wide[j * LAYERS + k] = jnp.broadcast_to(speeds[k:k + 1, :], (SUB, width))
            rwide[j * LAYERS + k] = jnp.broadcast_to(slow[k:k + 1, :], (SUB, width))

    smalls[0].wait()
    smalls[1].wait()
    index = vidx[...]
    speed = jnp.zeros(index.shape, jnp.float32)
    for i in range(vtab.shape[1]):
        speed = jnp.where(index == i, vtab[:, i:i + 1], speed)
    vel[0] = speed
    spread_rows(0)

    pl.semaphore_wait(barrier, 6)

    def vel_copy(j):
        return pltpu.make_async_remote_copy(
            src_ref=vel.at[0], dst_ref=vel.at[j], send_sem=vsend.at[j], recv_sem=vrecv.at[j],
            device_id=at(-j), device_id_type=pl.DeviceIdType.MESH)

    vel_copy(1).start()
    vel_copy(2).start()

    for copy in smalls[2:]:
        copy.wait()
    wb[0] = jnp.broadcast_to(as_column(fang[...]), (FB, LANE))
    cacc[...] = jnp.zeros_like(cacc)

    @pl.when(has_top)
    def _():
        wb[1] = jnp.broadcast_to(as_column(sang[pl.ds(tick, 1), :]), (FB, LANE))
        cell = lax.broadcasted_iota(jnp.int32, (FB, width), 1)
        pair = wav[tick]
        for i in range(2):
            field[1, i] = jnp.where(cell == spos[...], as_column(pair[i:i + 1, :]), 0.0)
        rec_copy.wait()
        values = recbuf[...].reshape(2 * FB, recbuf.shape[2])
        high = values.astype(jnp.bfloat16)
        rest = values - high.astype(jnp.float32)
        mid = rest.astype(jnp.bfloat16)
        low = (rest - mid.astype(jnp.float32)).astype(jnp.bfloat16)
        parts = jnp.concatenate([high, mid, low], axis=0)
        where_to = rpos[...]
        block = 2 * LANE

        def place(i, carry):
            first = pl.multiple_of(i * block, block)
            x = lax.broadcasted_iota(jnp.int32, (block, where_to.shape[1]), 0) + first
            hit = jnp.where(x == where_to, 1.0, 0.0).astype(jnp.bfloat16)
            got = lax.dot_general(parts, hit, (((1,), (1,)), ((), ())), preferred_element_type=jnp.float32)
            total = got[:2 * FB] + (got[2 * FB:4 * FB] + got[4 * FB:])
            field[1, 2:4, :, pl.ds(first, block)] = total.reshape(2, FB, block)
            return carry

        lax.fori_loop(0, width // block, place, 0)

    top_copy = pltpu.make_async_copy(field.at[1], fout.at[0], top_sem.at[0])

    @pl.when(d == 0)
    def _():
        top_copy.start()

    lane = lax.broadcasted_iota(jnp.int32, (SUB, LANE), 1)
    zero = jnp.zeros((SUB, LANE), jnp.float32)

    def layer(b, g, j, l):
        rows = pl.ds(pl.multiple_of(g * SUB, SUB), SUB)
        w = wb[b, rows, :]
        gain_w = (lateral_scale * 16.0 / 24.0) / w
        keep_l1, keep_l2 = lane < 1, lane < 2
        keep_r1, keep_r2 = lane >= LANE - 1, lane >= LANE - 2

        def rotated(c):
            span = pl.ds(c * LANE, LANE)
            p = w * rwide[j * LAYERS + l, :, span]
            y = p * p
            co = poly(y, COS)
            si = p * poly(y, SINC)
            sr, sm = field[b, 0, rows, span], field[b, 1, rows, span]
            rr, rm = field[b, 2, rows, span], field[b, 3, rows, span]
            u = (sr * co - sm * si, sr * si + sm * co, rr * co + rm * si, rm * co - rr * si)
            return [(v, pltpu.roll(v, 1, 1), pltpu.roll(v, 2, 1), pltpu.roll(v, LANE - 1, 1), pltpu.roll(v, LANE - 2, 1)) for v in u]

        outside = [(zero,) * 5] * 4
        before, here = outside, rotated(0)
        for c in range(cols):
            after = rotated(c + 1) if c + 1 < cols else outside
            span = pl.ds(c * LANE, LANE)
            spread = []
            for q in range(4):
                left1 = jnp.where(keep_l1, before[q][1], here[q][1])
                left2 = jnp.where(keep_l2, before[q][2], here[q][2])
                right1 = jnp.where(keep_r1, after[q][3], here[q][3])
                right2 = jnp.where(keep_r2, after[q][4], here[q][4])
                spread.append((left1 + right1) - (left2 + right2) * (1.0 / 16.0) - here[q][0] * 1.875)
            gain = gain_w * wide[j * LAYERS + l, :, span]
            damp = gain * damping
            new = (
                here[0][0] + (damp * spread[0] - gain * spread[1]),
                here[1][0] + (damp * spread[1] + gain * spread[0]),
                here[2][0] + (damp * spread[2] + gain * spread[3]),
                here[3][0] + (damp * spread[3] - gain * spread[2]),
            )
            for q in range(4):
                field[b, q, rows, span] = new[q]
            k = j * LAYERS + l
            cacc[k, :, span] = cacc[k, :, span] + (new[0] * new[2] + new[1] * new[3])
            before, here = here, after

    first = jnp.where(d >= n - 2, n - d, 0)
    sent = jnp.where(d >= n - 2, 1, 0)

    def out_copy(g):
        rows = pl.ds(pl.multiple_of(g * SUB, SUB), SUB)
        return pltpu.make_async_remote_copy(
            src_ref=field.at[sent, :, rows, :], dst_ref=fout.at[0, :, rows, :],
            send_sem=fsend.at[g], recv_sem=frecv.at[g],
            device_id=at(3), device_id_type=pl.DeviceIdType.MESH)

    def await_speed(j):
        vel_copy(j).wait_recv()
        spread_rows(j)

    def layers(b, g, j):
        def one(l, carry):
            layer(b, g, j, l)
            return carry

        lax.fori_loop(0, LAYERS, one, 0)

    def leaving(g, carry):
        @pl.when(first == 0)
        def _():
            fin_copy(g).wait()

        def slab(j, carry):
            @pl.when(jnp.logical_and(g == 0, j > 0))
            def _():
                await_speed(j)

            layers(sent, g, j)
            return carry

        lax.fori_loop(first, TICKS, slab, 0)

        @pl.when(d != n - 3)
        def _():
            out_copy(g).start()

        return carry

    lax.fori_loop(0, GROUPS, leaving, 0)

    joined = [jnp.where(lax.rem(d + k, n) == 0, 0.0, 0.5).astype(jnp.float32) for k in range(4)]
    last = TICKS * LAYERS
    last = TICKS * LAYERS

    def filter_rows(slabs):
        rows = {k: jnp.sum(cacc[k], axis=0, keepdims=True) * (1.0 / math.sqrt(FB))
                for j in range(TICKS) for k in range(LAYERS * j - 1, LAYERS * j + LAYERS + 1) if j in slabs and 0 <= k < last}

        def filtered(k):
            total = 2.0 * rows[k]
            if k > 0:
                total = total - (joined[k // LAYERS] if k % LAYERS == 0 else 0.5) * rows[k - 1]
            if k + 1 < last:
                total = total - (joined[(k + 1) // LAYERS] if (k + 1) % LAYERS == 0 else 0.5) * rows[k + 1]
            return total

        for j in slabs:
            for k in range(LAYERS):
                (own4, dn4, dn8)[j][pl.ds(k, 1), :] = filtered(j * LAYERS + k)
        if 0 in slabs:
            up1[...] = -joined[0] * rows[0]
        if 2 in slabs:
            dn12[...] = -joined[3] * rows[last - 1]

    image_copies = [
        pltpu.make_async_remote_copy(
            src_ref=src, dst_ref=dst, send_sem=isend.at[i], recv_sem=irecv.at[i],
            device_id=at(k), device_id_type=pl.DeviceIdType.MESH)
        for i, (src, dst, k) in enumerate(((up1, in_up, -1), (dn4, in_dn4, 1), (dn8, in_dn8, 2), (dn12, in_dn12, 3)))
    ]
    filter_rows((2,))
    image_copies[2].start()
    image_copies[3].start()

    @pl.when(first < 2)
    def _():
        filter_rows((1,))
        image_copies[1].start()

    @pl.when(first > 0)
    def _():
        def staying(g, carry):
            fin_copy(g).wait()

            def slab(j, carry):
                @pl.when(jnp.logical_and(g == 0, j > 0))
                def _():
                    await_speed(j)

                layers(0, g, j)
                return carry

            return lax.fori_loop(0, first, slab, carry)

        lax.fori_loop(0, GROUPS, staying, 0)

    @pl.when(first == 2)
    def _():
        filter_rows((1,))
        image_copies[1].start()

    filter_rows((0,))
    image_copies[0].start()
    for copy in image_copies:
        copy.wait()
    section[...] = own4[...] + in_dn4[...] + in_dn8[...]
    section[0:1, :] = section[0:1, :] + in_dn12[...]
    section[LAYERS - 1:LAYERS, :] = section[LAYERS - 1:LAYERS, :] + in_up[...]

    section_copy = pltpu.make_async_copy(section, section_out, small_sem.at[0])
    section_copy.start()
    section_copy.wait()
    vel_copy(1).wait_send()
    vel_copy(2).wait_send()

    @pl.when(d != n - 3)
    def _():
        for g in range(GROUPS):
            out_copy(g).wait_send()

    @pl.when(d != 0)
    def _():
        for g in range(GROUPS):
            out_copy(g).wait_recv()

    @pl.when(d == 0)
    def _():
        top_copy.wait()


def on_device(n, fields_in, flight_angular, wavelet, surface_angular, records, source_pos, receiver_pos, vel_table, vel_index):
    width = fields_in.shape[3]
    f32 = jnp.float32
    hbm = pl.BlockSpec(memory_space=pltpu.HBM)
    dma = pltpu.SemaphoreType.DMA
    last = TICKS * LAYERS
    fields_out, section = pl.pallas_call(
        functools.partial(kernel, n),
        out_shape=(
            jax.ShapeDtypeStruct(fields_in.shape, f32),
            jax.ShapeDtypeStruct((LAYERS, width), f32),
        ),
        in_specs=[hbm] * 9,
        out_specs=(hbm, hbm),
        scratch_shapes=[
            pltpu.VMEM(flight_angular.shape, f32),
            pltpu.VMEM(wavelet.shape, f32),
            pltpu.VMEM(surface_angular.shape, f32),
            pltpu.VMEM((1, 1), jnp.int32),
            pltpu.VMEM((1, receiver_pos.shape[0]), jnp.int32),
            pltpu.VMEM(vel_table.shape, f32),
            pltpu.VMEM(vel_index.shape, jnp.int32),
            pltpu.VMEM((LAYERS, width), f32),
            pltpu.VMEM((2, 4, FB, width), f32),
            pltpu.VMEM(records.shape[1:], f32),
            pltpu.VMEM((2, FB, LANE), f32),
            pltpu.VMEM((TICKS, LAYERS, width), f32),
            pltpu.VMEM((last, SUB, width), f32),
            pltpu.VMEM((last, SUB, width), f32),
            pltpu.VMEM((last, SUB, width), f32),
            pltpu.VMEM((1, width), f32),
            pltpu.VMEM((LAYERS, width), f32),
            pltpu.VMEM((LAYERS, width), f32),
            pltpu.VMEM((LAYERS, width), f32),
            pltpu.VMEM((1, width), f32),
            pltpu.VMEM((1, width), f32),
            pltpu.VMEM((LAYERS, width), f32),
            pltpu.VMEM((LAYERS, width), f32),
            pltpu.VMEM((1, width), f32),
            dma((7,)), dma((GROUPS,)), dma((1,)), dma((1,)), dma((TICKS,)), dma((TICKS,)),
            dma((GROUPS,)), dma((GROUPS,)), dma((4,)), dma((4,)),
        ],
        compiler_params=pltpu.CompilerParams(
            collective_id=0, has_side_effects=True, vmem_limit_bytes=62 * 1024 * 1024),
        name="migrate",
    )(fields_in, flight_angular, wavelet, surface_angular, records, source_pos.reshape(1, 1), receiver_pos.reshape(1, -1), vel_table, vel_index)
    return section, fields_out


def solution(mesh):
    placed = (
        P("depth", None, "shots", None),
        P("depth", "shots"),
        P(None, None, "shots"),
        P(None, "shots"),
        P(None, None, "shots", None),
        P("shots"),
        P("shots"),
        P("depth", None),
        P("depth", None),
    )
    return jax.shard_map(
        functools.partial(on_device, mesh.shape["depth"]),
        mesh=mesh,
        in_specs=placed,
        out_specs=(P("depth", "shots"), P("depth", None, "shots", None)),
        check_vma=False,
    )
```

```python
import functools
import math

import jax
import jax.numpy as jnp
from jax import lax
from jax.experimental import pallas as pl
from jax.experimental.pallas import tpu as pltpu
from jax.sharding import PartitionSpec as P

FB = 32
TICKS = 3
LAYERS = 4
SUB = 8
LANE = 128
GROUPS = FB // SUB

lateral_scale = 0.03
damping = 0.3

COS = (1.0, -0.4999999403953552, 0.041666459292173386, -0.0013886659871786833, 2.4693899831618182e-05, -2.514234438422136e-07)
SINC = (0.9999999403953552, -0.16666607558727264, 0.008332140743732452, -0.00019757583504542708, 2.5143860966636566e-06)


def poly(y, coefs):
    acc = coefs[-1] * y + coefs[-2]
    for c in coefs[-3::-1]:
        acc = acc * y + c
    return acc


def as_column(row):
    size = row.shape[1]
    diag = lax.broadcasted_iota(jnp.int32, (size, size), 0) == lax.broadcasted_iota(jnp.int32, (size, size), 1)
    return jnp.sum(jnp.where(diag, row, 0.0), axis=1, keepdims=True)


def kernel(
    n, fin, fang_in, wav_in, sang_in, rec, spos_in, rpos_in, vtab_in, vidx_in,
    fout, section_out,
    fang, wav, sang, spos, rpos, vtab, vidx, section,
    field, recbuf, wb, vel, wide, rwide, cacc, up1, own4, dn4, dn8, dn12, in_up, in_dn4, in_dn8, in_dn12, top4, in_top4, top8, in_top8,
    small_sem, fin_sem, rec_sem, top_sem, vsend, vrecv, fsend, frecv, isend, irecv,
):
    width = fin.shape[3]
    cols = width // LANE
    d = lax.axis_index("depth")

    def at(k):
        return {"depth": lax.rem(d + k + n, n)}

    def there(k):
        return d + k < n if k > 0 else d + k >= 0

    barrier = pltpu.get_barrier_semaphore()
    for k in (1, 2, 3, -1, -2, -3):
        @pl.when(there(k))
        def _():
            pl.semaphore_signal(barrier, inc=1, device_id=at(k), device_id_type=pl.DeviceIdType.MESH)

    smalls = [
        pltpu.make_async_copy(src, dst, small_sem.at[i])
        for i, (src, dst) in enumerate((
            (vidx_in, vidx), (vtab_in, vtab), (fang_in, fang), (sang_in, sang), (wav_in, wav), (spos_in, spos), (rpos_in, rpos)))
    ]
    for copy in smalls:
        copy.start()

    def fin_copy(g):
        rows = pl.ds(pl.multiple_of(g * SUB, SUB), SUB)
        return pltpu.make_async_copy(fin.at[0, :, rows, :], field.at[0, :, rows, :], fin_sem.at[g])

    for g in range(GROUPS):
        fin_copy(g).start()

    has_top = d < TICKS
    tick = jnp.maximum(TICKS - 1 - d, 0)
    rec_copy = pltpu.make_async_copy(rec.at[tick], recbuf, rec_sem.at[0])

    @pl.when(has_top)
    def _():
        rec_copy.start()

    def spread_rows(j):
        speeds = vel[j]
        slow = 1.0 / speeds
        for k in range(LAYERS):
            wide[j * LAYERS + k] = jnp.broadcast_to(speeds[k:k + 1, :], (SUB, width))
            rwide[j * LAYERS + k] = jnp.broadcast_to(slow[k:k + 1, :], (SUB, width))

    smalls[0].wait()
    smalls[1].wait()
    index = vidx[...]
    speed = jnp.zeros(index.shape, jnp.float32)
    for i in range(vtab.shape[1]):
        speed = jnp.where(index == i, vtab[:, i:i + 1], speed)
    vel[0] = speed
    spread_rows(0)

    pl.semaphore_wait(barrier, jnp.minimum(d, 3) + jnp.minimum(n - 1 - d, 3))

    def vel_copy(j):
        return pltpu.make_async_remote_copy(
            src_ref=vel.at[0], dst_ref=vel.at[j], send_sem=vsend.at[j], recv_sem=vrecv.at[j],
            device_id=at(jnp.where(j < TICKS, -j, 5 - j)), device_id_type=pl.DeviceIdType.MESH)

    speed_sent = ((1, d >= 1), (2, d >= 2), (4, d <= 1), (3, d == 0))
    for j, sends in speed_sent:
        @pl.when(sends)
        def _(j=j):
            vel_copy(j).start()

    for copy in smalls[2:]:
        copy.wait()
    wb[0] = jnp.broadcast_to(as_column(fang[...]), (FB, LANE))
    cacc[...] = jnp.zeros_like(cacc)

    @pl.when(has_top)
    def _():
        wb[1] = jnp.broadcast_to(as_column(sang[pl.ds(tick, 1), :]), (FB, LANE))
        cell = lax.broadcasted_iota(jnp.int32, (FB, width), 1)
        pair = wav[tick]
        for i in range(2):
            field[1, i] = jnp.where(cell == spos[...], as_column(pair[i:i + 1, :]), 0.0)
        rec_copy.wait()
        values = recbuf[...].reshape(2 * FB, recbuf.shape[2])
        high = values.astype(jnp.bfloat16)
        rest = values - high.astype(jnp.float32)
        mid = rest.astype(jnp.bfloat16)
        low = (rest - mid.astype(jnp.float32)).astype(jnp.bfloat16)
        parts = jnp.concatenate([high, mid, low], axis=0)
        where_to = rpos[...]
        block = 2 * LANE

        def place(i, carry):
            first = pl.multiple_of(i * block, block)
            x = lax.broadcasted_iota(jnp.int32, (block, where_to.shape[1]), 0) + first
            hit = jnp.where(x == where_to, 1.0, 0.0).astype(jnp.bfloat16)
            got = lax.dot_general(parts, hit, (((1,), (1,)), ((), ())), preferred_element_type=jnp.float32)
            total = got[:2 * FB] + (got[2 * FB:4 * FB] + got[4 * FB:])
            field[1, 2:4, :, pl.ds(first, block)] = total.reshape(2, FB, block)
            return carry

        lax.fori_loop(0, width // block, place, 0)

    def top_part(g):
        rows = pl.ds(pl.multiple_of(g * SUB, SUB), SUB)
        return pltpu.make_async_copy(field.at[1, :, rows, :], fout.at[0, :, rows, :], top_sem.at[g])

    @pl.when(d == 0)
    def _():
        for g in range(GROUPS):
            top_part(g).start()

    lane = lax.broadcasted_iota(jnp.int32, (SUB, LANE), 1)
    zero = jnp.zeros((SUB, LANE), jnp.float32)

    def layer(b, g, j, l):
        rows = pl.ds(pl.multiple_of(g * SUB, SUB), SUB)
        w = wb[b, rows, :]
        gain_w = (lateral_scale * 16.0 / 24.0) / w
        keep_l1, keep_l2 = lane < 1, lane < 2
        keep_r1, keep_r2 = lane >= LANE - 1, lane >= LANE - 2

        def rotated(c):
            span = pl.ds(c * LANE, LANE)
            p = w * rwide[j * LAYERS + l, :, span]
            y = p * p
            co = poly(y, COS)
            si = p * poly(y, SINC)
            sr, sm = field[b, 0, rows, span], field[b, 1, rows, span]
            rr, rm = field[b, 2, rows, span], field[b, 3, rows, span]
            u = (sr * co - sm * si, sr * si + sm * co, rr * co + rm * si, rm * co - rr * si)
            return [(v, pltpu.roll(v, 1, 1), pltpu.roll(v, 2, 1), pltpu.roll(v, LANE - 1, 1), pltpu.roll(v, LANE - 2, 1)) for v in u]

        outside = [(zero,) * 5] * 4
        before, here = outside, rotated(0)
        for c in range(cols):
            after = rotated(c + 1) if c + 1 < cols else outside
            span = pl.ds(c * LANE, LANE)
            spread = []
            for q in range(4):
                left1 = jnp.where(keep_l1, before[q][1], here[q][1])
                left2 = jnp.where(keep_l2, before[q][2], here[q][2])
                right1 = jnp.where(keep_r1, after[q][3], here[q][3])
                right2 = jnp.where(keep_r2, after[q][4], here[q][4])
                spread.append((left1 + right1) - (left2 + right2) * (1.0 / 16.0) - here[q][0] * 1.875)
            gain = gain_w * wide[j * LAYERS + l, :, span]
            damp = gain * damping
            new = (
                here[0][0] + (damp * spread[0] - gain * spread[1]),
                here[1][0] + (damp * spread[1] + gain * spread[0]),
                here[2][0] + (damp * spread[2] + gain * spread[3]),
                here[3][0] + (damp * spread[3] - gain * spread[2]),
            )
            for q in range(4):
                field[b, q, rows, span] = new[q]
            k = j * LAYERS + l
            cacc[k, :, span] = cacc[k, :, span] + (new[0] * new[2] + new[1] * new[3])
            before, here = here, after

    def out_copy(g):
        rows = pl.ds(pl.multiple_of(g * SUB, SUB), SUB)
        return pltpu.make_async_remote_copy(
            src_ref=field.at[0, :, rows, :], dst_ref=fout.at[0, :, rows, :],
            send_sem=fsend.at[g], recv_sem=frecv.at[g],
            device_id=at(3), device_id_type=pl.DeviceIdType.MESH)

    def await_speed(j):
        vel_copy(j).wait_recv()
        spread_rows(j)

    def layers(b, g, j):
        def one(l, carry):
            layer(b, g, j, l)
            return carry

        lax.fori_loop(0, LAYERS, one, 0)

    def leaving(g, carry):
        fin_copy(g).wait()

        def slab(j, carry):
            @pl.when(jnp.logical_and(g == 0, j > 0))
            def _():
                await_speed(j)

            layers(0, g, j)
            return carry

        lax.fori_loop(0, jnp.minimum(TICKS, n - d), slab, 0)

        @pl.when(d + 3 < n)
        def _():
            out_copy(g).start()

        return carry

    lax.fori_loop(0, GROUPS, leaving, 0)

    joined = [jnp.where(jnp.logical_and(d + k > 0, d + k < n), 0.5, 0.0).astype(jnp.float32) for k in range(4)]
    last = TICKS * LAYERS

    def filter_rows(slabs):
        rows = {k: jnp.sum(cacc[k], axis=0, keepdims=True) * (1.0 / math.sqrt(FB))
                for j in range(TICKS) for k in range(LAYERS * j - 1, LAYERS * j + LAYERS + 1) if j in slabs and 0 <= k < last}

        def filtered(k):
            total = 2.0 * rows[k]
            if k > 0:
                total = total - (joined[k // LAYERS] if k % LAYERS == 0 else 0.5) * rows[k - 1]
            if k + 1 < last:
                total = total - (joined[(k + 1) // LAYERS] if (k + 1) % LAYERS == 0 else 0.5) * rows[k + 1]
            return total

        for j in slabs:
            for k in range(LAYERS):
                (own4, dn4, dn8)[j][pl.ds(k, 1), :] = filtered(j * LAYERS + k)
        if 0 in slabs:
            up1[...] = -joined[0] * rows[0]
        if 2 in slabs:
            dn12[...] = -joined[3] * rows[last - 1]

    image_copies = [
        pltpu.make_async_remote_copy(
            src_ref=src, dst_ref=dst, send_sem=isend.at[i], recv_sem=irecv.at[i],
            device_id=at(k), device_id_type=pl.DeviceIdType.MESH)
        for i, (src, dst, k) in enumerate(((up1, in_up, -1), (dn4, in_dn4, 1), (dn8, in_dn8, 2), (dn12, in_dn12, 3), (top4, in_top4, -1), (top8, in_top8, -2)))
    ]
    moves = [
        (image_copies[0], d >= 1, d + 1 < n),
        (image_copies[1], d + 1 < n, d >= 1),
        (image_copies[2], d + 2 < n, d >= 2),
        (image_copies[3], d + 3 < n, d >= 3),
        (image_copies[4], jnp.logical_or(d == 1, d == 2), d <= 1),
        (image_copies[5], d == 2, d == 0),
    ]
    filter_rows((0, 1, 2))
    for copy, sends, _ in moves[:4]:
        @pl.when(sends)
        def _(copy=copy):
            copy.start()

    section[...] = own4[...]

    @pl.when(jnp.logical_or(d == 1, d == 2))
    def _():
        def passing(g, carry):
            def slab(j, carry):
                @pl.when(g == 0)
                def _():
                    await_speed(j)

                layers(1, g, j)
                return carry

            lax.fori_loop(5 - d, 5, slab, 0)
            top_part(g).start()
            return carry

        lax.fori_loop(0, GROUPS, passing, 0)
        above = [jnp.sum(cacc[last + k], axis=0, keepdims=True) * (1.0 / math.sqrt(FB)) for k in range(2 * LAYERS)]
        for k in range(2 * LAYERS):
            total = 2.0 * above[k]
            if k > 0:
                total = total - 0.5 * above[k - 1]
            if k + 1 < 2 * LAYERS:
                total = total - 0.5 * above[k + 1]
            (top8 if k < LAYERS else top4)[pl.ds(k % LAYERS, 1), :] = total
        section[0:1, :] = section[0:1, :] - 0.5 * above[-1]

    for copy, sends, _ in moves[4:]:
        @pl.when(sends)
        def _(copy=copy):
            copy.start()

    for (copy, sends, gets), landed, at_row in zip(
            moves, (in_up, in_dn4, in_dn8, in_dn12, in_top4, in_top8), (LAYERS - 1, None, None, 0, None, None)):
        @pl.when(sends)
        def _(copy=copy):
            copy.wait_send()

        @pl.when(gets)
        def _(copy=copy, landed=landed, at_row=at_row):
            copy.wait_recv()
            if at_row is None:
                section[...] = section[...] + landed[...]
            else:
                section[at_row:at_row + 1, :] = section[at_row:at_row + 1, :] + landed[...]

    section_copy = pltpu.make_async_copy(section, section_out, small_sem.at[0])
    section_copy.start()
    section_copy.wait()
    for j, sends in speed_sent:
        @pl.when(sends)
        def _(j=j):
            vel_copy(j).wait_send()

    @pl.when(d + 3 < n)
    def _():
        for g in range(GROUPS):
            out_copy(g).wait_send()

    @pl.when(d >= 3)
    def _():
        for g in range(GROUPS):
            out_copy(g).wait_recv()

    @pl.when(d < TICKS)
    def _():
        for g in range(GROUPS):
            top_part(g).wait()


def on_device(n, fields_in, flight_angular, wavelet, surface_angular, records, source_pos, receiver_pos, vel_table, vel_index):
    width = fields_in.shape[3]
    f32 = jnp.float32
    hbm = pl.BlockSpec(memory_space=pltpu.HBM)
    dma = pltpu.SemaphoreType.DMA
    last = TICKS * LAYERS
    fields_out, section = pl.pallas_call(
        functools.partial(kernel, n),
        out_shape=(
            jax.ShapeDtypeStruct(fields_in.shape, f32),
            jax.ShapeDtypeStruct((LAYERS, width), f32),
        ),
        in_specs=[hbm] * 9,
        out_specs=(hbm, hbm),
        scratch_shapes=[
            pltpu.VMEM(flight_angular.shape, f32),
            pltpu.VMEM(wavelet.shape, f32),
            pltpu.VMEM(surface_angular.shape, f32),
            pltpu.VMEM((1, 1), jnp.int32),
            pltpu.VMEM((1, receiver_pos.shape[0]), jnp.int32),
            pltpu.VMEM(vel_table.shape, f32),
            pltpu.VMEM(vel_index.shape, jnp.int32),
            pltpu.VMEM((LAYERS, width), f32),
            pltpu.VMEM((2, 4, FB, width), f32),
            pltpu.VMEM(records.shape[1:], f32),
            pltpu.VMEM((2, FB, LANE), f32),
            pltpu.VMEM((5, LAYERS, width), f32),
            pltpu.VMEM((5 * LAYERS, SUB, width), f32),
            pltpu.VMEM((5 * LAYERS, SUB, width), f32),
            pltpu.VMEM((5 * LAYERS, SUB, width), f32),
            pltpu.VMEM((1, width), f32),
            pltpu.VMEM((LAYERS, width), f32),
            pltpu.VMEM((LAYERS, width), f32),
            pltpu.VMEM((LAYERS, width), f32),
            pltpu.VMEM((1, width), f32),
            pltpu.VMEM((1, width), f32),
            pltpu.VMEM((LAYERS, width), f32),
            pltpu.VMEM((LAYERS, width), f32),
            pltpu.VMEM((1, width), f32),
            pltpu.VMEM((LAYERS, width), f32),
            pltpu.VMEM((LAYERS, width), f32),
            pltpu.VMEM((LAYERS, width), f32),
            pltpu.VMEM((LAYERS, width), f32),
            dma((7,)), dma((GROUPS,)), dma((1,)), dma((GROUPS,)), dma((5,)), dma((5,)),
            dma((GROUPS,)), dma((GROUPS,)), dma((6,)), dma((6,)),
        ],
        compiler_params=pltpu.CompilerParams(
            collective_id=0, has_side_effects=True, vmem_limit_bytes=62 * 1024 * 1024),
        name="migrate",
    )(fields_in, flight_angular, wavelet, surface_angular, records, source_pos.reshape(1, 1), receiver_pos.reshape(1, -1), vel_table, vel_index)
    return section, fields_out


def solution(mesh):
    placed = (
        P("depth", None, "shots", None),
        P("depth", "shots"),
        P(None, None, "shots"),
        P(None, "shots"),
        P(None, None, "shots", None),
        P("shots"),
        P("shots"),
        P("depth", None),
        P("depth", None),
    )
    return jax.shard_map(
        functools.partial(on_device, mesh.shape["depth"]),
        mesh=mesh,
        in_specs=placed,
        out_specs=(P("depth", "shots"), P("depth", None, "shots", None)),
        check_vma=False,
    )
```

```python
import functools
import math

import jax
import jax.numpy as jnp
from jax import lax
from jax.experimental import pallas as pl
from jax.experimental.pallas import tpu as pltpu
from jax.sharding import PartitionSpec as P

FB = 32
TICKS = 3
LAYERS = 4
SUB = 8
LANE = 128
GROUPS = FB // SUB

lateral_scale = 0.03
damping = 0.3

COS = (1.0, -0.4999999403953552, 0.041666459292173386, -0.0013886659871786833, 2.4693899831618182e-05, -2.514234438422136e-07)
SINC = (0.9999999403953552, -0.16666607558727264, 0.008332140743732452, -0.00019757583504542708, 2.5143860966636566e-06)


def poly(y, coefs):
    acc = coefs[-1] * y + coefs[-2]
    for c in coefs[-3::-1]:
        acc = acc * y + c
    return acc


def as_column(row):
    size = row.shape[1]
    diag = lax.broadcasted_iota(jnp.int32, (size, size), 0) == lax.broadcasted_iota(jnp.int32, (size, size), 1)
    return jnp.sum(jnp.where(diag, row, 0.0), axis=1, keepdims=True)


def kernel(
    n, fin, fang_in, wav_in, sang_in, rec, spos_in, rpos_in, vtab_in, vidx_in,
    fout, section_out,
    fang, wav, sang, spos, rpos, vtab, vidx, section,
    field, recbuf, wb, vel, wide, rwide, cacc, up1, own4, dn4, dn8, dn12, in_up, in_dn4, in_dn8, in_dn12,
    small_sem, fin_sem, rec_sem, top_sem, vsend, vrecv, fsend, frecv, isend, irecv,
):
    width = fin.shape[3]
    cols = width // LANE
    d = lax.axis_index("depth")

    def at(k):
        return {"depth": lax.rem(d + k + n, n)}

    barrier = pltpu.get_barrier_semaphore()
    for k in (1, 2, 3, -1, -2, -3):
        pl.semaphore_signal(barrier, inc=1, device_id=at(k), device_id_type=pl.DeviceIdType.MESH)

    smalls = [
        pltpu.make_async_copy(src, dst, small_sem.at[i])
        for i, (src, dst) in enumerate((
            (vidx_in, vidx), (vtab_in, vtab), (fang_in, fang), (sang_in, sang), (wav_in, wav), (spos_in, spos), (rpos_in, rpos)))
    ]
    for copy in smalls:
        copy.start()

    def fin_copy(g):
        rows = pl.ds(pl.multiple_of(g * SUB, SUB), SUB)
        return pltpu.make_async_copy(fin.at[0, :, rows, :], field.at[0, :, rows, :], fin_sem.at[g])

    for g in range(GROUPS):
        fin_copy(g).start()

    has_top = jnp.logical_or(d == 0, d >= n - 2)
    tick = jnp.where(d == 0, TICKS - 1, lax.rem(n - 1 - d, TICKS))
    rec_copy = pltpu.make_async_copy(rec.at[tick], recbuf, rec_sem.at[0])

    @pl.when(has_top)
    def _():
        rec_copy.start()

    def spread_rows(j):
        speeds = vel[j]
        slow = 1.0 / speeds
        for k in range(LAYERS):
            wide[j * LAYERS + k] = jnp.broadcast_to(speeds[k:k + 1, :], (SUB, width))
            rwide[j * LAYERS + k] = jnp.broadcast_to(slow[k:k + 1, :], (SUB, width))

    smalls[0].wait()
    smalls[1].wait()
    index = vidx[...]
    speed = jnp.zeros(index.shape, jnp.float32)
    for i in range(vtab.shape[1]):
        speed = jnp.where(index == i, vtab[:, i:i + 1], speed)
    vel[0] = speed
    spread_rows(0)

    pl.semaphore_wait(barrier, 6)

    def vel_copy(j):
        return pltpu.make_async_remote_copy(
            src_ref=vel.at[0], dst_ref=vel.at[j], send_sem=vsend.at[j], recv_sem=vrecv.at[j],
            device_id=at(-j), device_id_type=pl.DeviceIdType.MESH)

    vel_copy(1).start()
    vel_copy(2).start()

    for copy in smalls[2:]:
        copy.wait()
    wb[0] = jnp.broadcast_to(as_column(fang[...]), (FB, LANE))
    cacc[...] = jnp.zeros_like(cacc)

    @pl.when(has_top)
    def _():
        wb[1] = jnp.broadcast_to(as_column(sang[pl.ds(tick, 1), :]), (FB, LANE))
        cell = lax.broadcasted_iota(jnp.int32, (FB, width), 1)
        pair = wav[tick]
        for i in range(2):
            field[1, i] = jnp.where(cell == spos[...], as_column(pair[i:i + 1, :]), 0.0)
        rec_copy.wait()
        values = recbuf[...].reshape(2 * FB, recbuf.shape[2])
        high = values.astype(jnp.bfloat16)
        rest = values - high.astype(jnp.float32)
        mid = rest.astype(jnp.bfloat16)
        low = (rest - mid.astype(jnp.float32)).astype(jnp.bfloat16)
        parts = jnp.concatenate([high, mid, low], axis=0)
        where_to = rpos[...]
        block = 2 * LANE

        def place(i, carry):
            first = pl.multiple_of(i * block, block)
            x = lax.broadcasted_iota(jnp.int32, (block, where_to.shape[1]), 0) + first
            hit = jnp.where(x == where_to, 1.0, 0.0).astype(jnp.bfloat16)
            got = lax.dot_general(parts, hit, (((1,), (1,)), ((), ())), preferred_element_type=jnp.float32)
            total = got[:2 * FB] + (got[2 * FB:4 * FB] + got[4 * FB:])
            field[1, 2:4, :, pl.ds(first, block)] = total.reshape(2, FB, block)
            return carry

        lax.fori_loop(0, width // block, place, 0)

    top_copy = pltpu.make_async_copy(field.at[1], fout.at[0], top_sem.at[0])

    @pl.when(d == 0)
    def _():
        top_copy.start()

    lane = lax.broadcasted_iota(jnp.int32, (SUB, LANE), 1)
    zero = jnp.zeros((SUB, LANE), jnp.float32)

    def layer(b, g, j, l):
        rows = pl.ds(pl.multiple_of(g * SUB, SUB), SUB)
        w = wb[b, rows, :]
        gain_w = (lateral_scale * 16.0 / 24.0) / w
        keep_l1, keep_l2 = lane < 1, lane < 2
        keep_r1, keep_r2 = lane >= LANE - 1, lane >= LANE - 2

        def rotated(c):
            span = pl.ds(c * LANE, LANE)
            p = w * rwide[j * LAYERS + l, :, span]
            y = p * p
            co = poly(y, COS)
            si = p * poly(y, SINC)
            sr, sm = field[b, 0, rows, span], field[b, 1, rows, span]
            rr, rm = field[b, 2, rows, span], field[b, 3, rows, span]
            u = (sr * co - sm * si, sr * si + sm * co, rr * co + rm * si, rm * co - rr * si)
            return [(v, pltpu.roll(v, 1, 1), pltpu.roll(v, 2, 1), pltpu.roll(v, LANE - 1, 1), pltpu.roll(v, LANE - 2, 1)) for v in u]

        outside = [(zero,) * 5] * 4
        before, here = outside, rotated(0)
        for c in range(cols):
            after = rotated(c + 1) if c + 1 < cols else outside
            span = pl.ds(c * LANE, LANE)
            spread = []
            for q in range(4):
                left1 = jnp.where(keep_l1, before[q][1], here[q][1])
                left2 = jnp.where(keep_l2, before[q][2], here[q][2])
                right1 = jnp.where(keep_r1, after[q][3], here[q][3])
                right2 = jnp.where(keep_r2, after[q][4], here[q][4])
                spread.append((left1 + right1) - (left2 + right2) * (1.0 / 16.0) - here[q][0] * 1.875)
            gain = gain_w * wide[j * LAYERS + l, :, span]
            damp = gain * damping
            new = (
                here[0][0] + (damp * spread[0] - gain * spread[1]),
                here[1][0] + (damp * spread[1] + gain * spread[0]),
                here[2][0] + (damp * spread[2] + gain * spread[3]),
                here[3][0] + (damp * spread[3] - gain * spread[2]),
            )
            for q in range(4):
                field[b, q, rows, span] = new[q]
            k = j * LAYERS + l
            cacc[k, :, span] = cacc[k, :, span] + (new[0] * new[2] + new[1] * new[3])
            before, here = here, after

    first = jnp.where(d >= n - 2, n - d, 0)
    sent = jnp.where(d >= n - 2, 1, 0)

    def out_copy(g):
        rows = pl.ds(pl.multiple_of(g * SUB, SUB), SUB)
        return pltpu.make_async_remote_copy(
            src_ref=field.at[sent, :, rows, :], dst_ref=fout.at[0, :, rows, :],
            send_sem=fsend.at[g], recv_sem=frecv.at[g],
            device_id=at(3), device_id_type=pl.DeviceIdType.MESH)

    def await_speed(j):
        vel_copy(j).wait_recv()
        spread_rows(j)

    def layers(b, g, j):
        def one(l, carry):
            layer(b, g, j, l)
            return carry

        lax.fori_loop(0, LAYERS, one, 0)

    def leaving(g, carry):
        @pl.when(first == 0)
        def _():
            fin_copy(g).wait()

        def slab(j, carry):
            @pl.when(jnp.logical_and(g == 0, j > 0))
            def _():
                await_speed(j)

            layers(sent, g, j)
            return carry

        lax.fori_loop(first, TICKS, slab, 0)

        @pl.when(d != n - 3)
        def _():
            out_copy(g).start()

        return carry

    lax.fori_loop(0, GROUPS, leaving, 0)

    joined = [jnp.where(lax.rem(d + k, n) == 0, 0.0, 0.5).astype(jnp.float32) for k in range(4)]
    last = TICKS * LAYERS
    last = TICKS * LAYERS

    def filter_rows(slabs):
        rows = {k: jnp.sum(cacc[k], axis=0, keepdims=True) * (1.0 / math.sqrt(FB))
                for j in range(TICKS) for k in range(LAYERS * j - 1, LAYERS * j + LAYERS + 1) if j in slabs and 0 <= k < last}

        def filtered(k):
            total = 2.0 * rows[k]
            if k > 0:
                total = total - (joined[k // LAYERS] if k % LAYERS == 0 else 0.5) * rows[k - 1]
            if k + 1 < last:
                total = total - (joined[(k + 1) // LAYERS] if (k + 1) % LAYERS == 0 else 0.5) * rows[k + 1]
            return total

        for j in slabs:
            for k in range(LAYERS):
                (own4, dn4, dn8)[j][pl.ds(k, 1), :] = filtered(j * LAYERS + k)
        if 0 in slabs:
            up1[...] = -joined[0] * rows[0]
        if 2 in slabs:
            dn12[...] = -joined[3] * rows[last - 1]

    image_copies = [
        pltpu.make_async_remote_copy(
            src_ref=src, dst_ref=dst, send_sem=isend.at[i], recv_sem=irecv.at[i],
            device_id=at(k), device_id_type=pl.DeviceIdType.MESH)
        for i, (src, dst, k) in enumerate(((up1, in_up, -1), (dn4, in_dn4, 1), (dn8, in_dn8, 2), (dn12, in_dn12, 3)))
    ]
    filter_rows((2,))
    image_copies[2].start()
    image_copies[3].start()

    @pl.when(first < 2)
    def _():
        filter_rows((1,))
        image_copies[1].start()

    @pl.when(first > 0)
    def _():
        def staying(g, carry):
            fin_copy(g).wait()

            def slab(j, carry):
                @pl.when(jnp.logical_and(g == 0, j > 0))
                def _():
                    await_speed(j)

                layers(0, g, j)
                return carry

            return lax.fori_loop(0, first, slab, carry)

        lax.fori_loop(0, GROUPS, staying, 0)

    @pl.when(first == 2)
    def _():
        filter_rows((1,))
        image_copies[1].start()

    filter_rows((0,))
    image_copies[0].start()
    for copy in image_copies:
        copy.wait()
    section[...] = own4[...] + in_dn4[...] + in_dn8[...]
    section[0:1, :] = section[0:1, :] + in_dn12[...]
    section[LAYERS - 1:LAYERS, :] = section[LAYERS - 1:LAYERS, :] + in_up[...]

    section_copy = pltpu.make_async_copy(section, section_out, small_sem.at[0])
    section_copy.start()
    section_copy.wait()
    vel_copy(1).wait_send()
    vel_copy(2).wait_send()

    @pl.when(d != n - 3)
    def _():
        for g in range(GROUPS):
            out_copy(g).wait_send()

    @pl.when(d != 0)
    def _():
        for g in range(GROUPS):
            out_copy(g).wait_recv()

    @pl.when(d == 0)
    def _():
        top_copy.wait()


def on_device(n, fields_in, flight_angular, wavelet, surface_angular, records, source_pos, receiver_pos, vel_table, vel_index):
    width = fields_in.shape[3]
    f32 = jnp.float32
    hbm = pl.BlockSpec(memory_space=pltpu.HBM)
    dma = pltpu.SemaphoreType.DMA
    last = TICKS * LAYERS
    fields_out, section = pl.pallas_call(
        functools.partial(kernel, n),
        out_shape=(
            jax.ShapeDtypeStruct(fields_in.shape, f32),
            jax.ShapeDtypeStruct((LAYERS, width), f32),
        ),
        in_specs=[hbm] * 9,
        out_specs=(hbm, hbm),
        scratch_shapes=[
            pltpu.VMEM(flight_angular.shape, f32),
            pltpu.VMEM(wavelet.shape, f32),
            pltpu.VMEM(surface_angular.shape, f32),
            pltpu.VMEM((1, 1), jnp.int32),
            pltpu.VMEM((1, receiver_pos.shape[0]), jnp.int32),
            pltpu.VMEM(vel_table.shape, f32),
            pltpu.VMEM(vel_index.shape, jnp.int32),
            pltpu.VMEM((LAYERS, width), f32),
            pltpu.VMEM((2, 4, FB, width), f32),
            pltpu.VMEM(records.shape[1:], f32),
            pltpu.VMEM((2, FB, LANE), f32),
            pltpu.VMEM((TICKS, LAYERS, width), f32),
            pltpu.VMEM((last, SUB, width), f32),
            pltpu.VMEM((last, SUB, width), f32),
            pltpu.VMEM((last, SUB, width), f32),
            pltpu.VMEM((1, width), f32),
            pltpu.VMEM((LAYERS, width), f32),
            pltpu.VMEM((LAYERS, width), f32),
            pltpu.VMEM((LAYERS, width), f32),
            pltpu.VMEM((1, width), f32),
            pltpu.VMEM((1, width), f32),
            pltpu.VMEM((LAYERS, width), f32),
            pltpu.VMEM((LAYERS, width), f32),
            pltpu.VMEM((1, width), f32),
            dma((7,)), dma((GROUPS,)), dma((1,)), dma((1,)), dma((TICKS,)), dma((TICKS,)),
            dma((GROUPS,)), dma((GROUPS,)), dma((4,)), dma((4,)),
        ],
        compiler_params=pltpu.CompilerParams(
            collective_id=0, has_side_effects=True, vmem_limit_bytes=62 * 1024 * 1024),
        name="migrate",
    )(fields_in, flight_angular, wavelet, surface_angular, records, source_pos.reshape(1, 1), receiver_pos.reshape(1, -1), vel_table, vel_index)
    parts = 8

    def hand_over(fields_ref, section_ref, fields_to, section_to, sems):
        copies = [pltpu.make_async_copy(section_ref, section_to, sems.at[parts])]
        for i in range(parts):
            view = (0, i // 2, pl.ds(i % 2 * (FB // 2), FB // 2))
            copies.append(pltpu.make_async_copy(fields_ref.at[view], fields_to.at[view], sems.at[i]))
        for copy in copies:
            copy.start()
        for copy in copies:
            copy.wait()

    fields_out, section = pl.pallas_call(
        hand_over,
        out_shape=(jax.ShapeDtypeStruct(fields_out.shape, f32), jax.ShapeDtypeStruct(section.shape, f32)),
        in_specs=[hbm] * 2,
        out_specs=(hbm, hbm),
        scratch_shapes=[dma((parts + 1,))],
        compiler_params=pltpu.CompilerParams(vmem_limit_bytes=62 * 1024 * 1024),
        name="hand_over",
    )(fields_out, section)
    return section, fields_out


def solution(mesh):
    placed = (
        P("depth", None, "shots", None),
        P("depth", "shots"),
        P(None, None, "shots"),
        P(None, "shots"),
        P(None, None, "shots", None),
        P("shots"),
        P("shots"),
        P("depth", None),
        P("depth", None),
    )
    return jax.shard_map(
        functools.partial(on_device, mesh.shape["depth"]),
        mesh=mesh,
        in_specs=placed,
        out_specs=(P("depth", "shots"), P("depth", None, "shots", None)),
        check_vma=False,
    )
```
